32 devices in a mesh: batch: 8 (over y, x, core), seq: 4 (over z).
Axes of the slice: x: 2, y: 2, z: 4, core: 2. Of those that a mesh axis runs over, the one named last changes fastest.
Arguments:
- query_rows: bfloat16 [8, 2560, 3072], P('batch', 'seq'), may hold values from -16 to 16
- key_rows: bfloat16 [8, 2560, 3072], P('batch', 'seq'), may hold values from -16 to 16
- value_rows: bfloat16 [8, 2560, 3072], P('batch', 'seq'), may hold values from -10 to 10
- cached_rows: bfloat16 [8, 2560, 3072], P('batch', 'seq'), may hold values from -4 to 4
- plan: int32 [8, 28], replicated, may hold values from 0 to 1, as said below
- timestep: int32 [8], replicated, may hold values from 0 to 27
- assignment: int32 [8], replicated, may hold values from 0 to 7, as said below
Outputs:
- refreshed: bfloat16 [8, 2560, 3072], P('batch', 'seq')
The draws below stay inside these ranges and needn't reach their ends.
Inputs may be any that keep to these rules, and one draw needn't show every extreme that they name: plan[r, t] is 1 for t = 0 and for the timesteps at which request r refreshes, every 3 timesteps from its own offset, else 0. `assignment`: a permutation of the requests; of the two slots g and g + 4, exactly one holds a request with active = 1.
All inputs are finite; a program needn't handle non-finite values.
Results may differ from the reference program's by a relative error of at most 0.0025.
Values may be sent and summed in bfloat16 or wider, within the bound.
A program may use at most 128 MiB of HBM per device.

```python
import math
import jax
import jax.numpy as jnp
from jax import lax

HEADS = 24
HEAD_DIM = 128
D = 3072
SEQ_LEN = 2560
STEPS = 28
CACHE_EVERY = 3
REQUESTS = 8


def fora_tables(key):
    halfway = REQUESTS // 2
    base_key = jax.random.fold_in(key, 4242)
    order_seed, coin_seed, phase_seed, pick_seed = jax.random.split(base_key, 4)
    slot_order = jax.random.permutation(order_seed, REQUESTS).astype(jnp.int32)
    coin_flips = jax.random.randint(coin_seed, (halfway,), 0, 2).astype(jnp.int32)
    slot_full = jnp.concatenate([coin_flips, 1 - coin_flips])
    request_full = jnp.zeros((REQUESTS,), jnp.int32).at[slot_order].set(slot_full)
    phases = jax.random.randint(phase_seed, (REQUESTS,), 0, CACHE_EVERY).astype(jnp.int32)
    first_slot = jnp.where(coin_flips[0] == 1, 0, halfway)
    second_slot = jnp.where(coin_flips[1] == 1, 1, 1 + halfway)
    first_request = slot_order[first_slot]
    second_request = slot_order[second_slot]
    phases = phases.at[second_request].set(0)
    pick_values = jax.random.randint(pick_seed, (REQUESTS,), 0, 1 << 20).astype(jnp.int32)
    full_room = (STEPS - 1 + phases) // CACHE_EVERY
    reuse_room = (STEPS - 2 + phases) // CACHE_EVERY
    full_time = CACHE_EVERY * (1 + pick_values % full_room) - phases
    reuse_time = CACHE_EVERY * (1 + pick_values % reuse_room) - phases + 1
    step_times = jnp.where(request_full == 1, full_time, reuse_time).astype(jnp.int32)
    step_times = step_times.at[first_request].set(0).at[second_request].set(STEPS - 1)
    step_grid = jnp.arange(STEPS, dtype=jnp.int32)[None, :]
    refresh = (step_grid == 0) | ((step_grid + phases[:, None]) % CACHE_EVERY == 0)
    return (refresh.astype(jnp.int32), step_times, slot_order)


def draw_plan(key, part):
    return fora_tables(key)[0]


def draw_timestep(key, part):
    return fora_tables(key)[1]


def draw_assignment(key, part):
    return fora_tables(key)[2]


def query_key_pair(key):
    base_key = jax.random.fold_in(key, 777)
    query_seed, key_seed = jax.random.split(base_key, 2)
    queries = jnp.clip(1.41 * jax.random.normal(query_seed, (REQUESTS, SEQ_LEN, D), jnp.float32), -16.0, 16.0)
    keyrows = jnp.clip(1.41 * jax.random.normal(key_seed, (REQUESTS, SEQ_LEN, D), jnp.float32), -16.0, 16.0)
    return (queries, keyrows)


def draw_query_rows(key, part):
    return query_key_pair(key)[0].astype(jnp.bfloat16)


def draw_key_rows(key, part):
    return query_key_pair(key)[1].astype(jnp.bfloat16)


def levels(key, shape, cuts, smallest, top_value):
    factor_of = 1.0
    for dim, shards_of in cuts:
        heights = jax.random.uniform(jax.random.fold_in(jax.random.fold_in(key, 6), dim), (shards_of,), jnp.float32, smallest / len(cuts), top_value / len(cuts))
        factor_of = factor_of * jnp.repeat(jnp.exp(heights), shape[dim] // shards_of).reshape((-1,) + (1,) * (len(shape) - 1 - dim))
    return factor_of


def gaussian(stream_key, dims, scale, bound, pieces=(), kind=jnp.bfloat16):
    drawn = scale * jax.random.normal(stream_key, dims, jnp.float32)
    if pieces:
        drawn = drawn * levels(stream_key, dims, pieces, -0.22, 0.18)
    return jnp.clip(drawn, -bound, bound).astype(kind)


def setup_inputs(seed: int = 0) -> dict:
    splits = jax.random.split(jax.random.key(seed), 8)
    query_rows = draw_query_rows(jax.random.fold_in(splits[7], 71), 0)
    key_rows = draw_key_rows(jax.random.fold_in(splits[7], 71), 0)
    value_rows = gaussian(splits[2], (REQUESTS, SEQ_LEN, D), 2.0, 10.0, ((0, 8), (1, 4)))
    cached_rows = gaussian(splits[3], (REQUESTS, SEQ_LEN, D), 0.5, 4.0, ((0, 8), (1, 4)))
    plan = draw_plan(jax.random.fold_in(splits[7], 71), 0)
    timestep = draw_timestep(jax.random.fold_in(splits[7], 71), 0)
    assignment = draw_assignment(jax.random.fold_in(splits[7], 71), 0)
    return dict(query_rows=query_rows, key_rows=key_rows, value_rows=value_rows, cached_rows=cached_rows, plan=plan, timestep=timestep, assignment=assignment)


def attend_head(inputs):
    head_queries, head_keys, head_values = inputs
    factor = 1.0 / math.sqrt(head_queries.shape[-1])
    scores = jnp.dot(head_queries, head_keys.T, preferred_element_type=jnp.float32) * factor
    peak = lax.optimization_barrier(jnp.max(scores, axis=1, keepdims=True))
    shifted = jnp.exp(scores - peak)
    total = lax.optimization_barrier(jnp.sum(shifted, axis=1, keepdims=True))
    weights = shifted.astype(jnp.bfloat16)
    mixed = jnp.dot(weights, head_values, preferred_element_type=jnp.float32)
    return (mixed / total).astype(jnp.bfloat16)

def attend_request(query_rows, key_rows, value_rows):

    def split_heads(rows):
        return jnp.transpose(rows.reshape(SEQ_LEN, HEADS, HEAD_DIM), (1, 0, 2))
    heads_out = lax.map(attend_head, (split_heads(query_rows), split_heads(key_rows), split_heads(value_rows)))
    return jnp.transpose(heads_out, (1, 0, 2)).reshape(SEQ_LEN, HEADS * HEAD_DIM)

def reference(query_rows, key_rows, value_rows, cached_rows, plan, timestep, assignment):
    active = plan[assignment, timestep[assignment]] > 0

    def per_slot(inputs):
        slot_queries, slot_keys, slot_values, slot_cache, slot_flag = inputs

        def fresh(unused):
            return attend_request(slot_queries, slot_keys, slot_values)

        def reuse(unused):
            return slot_cache
        return lax.cond(slot_flag, fresh, reuse, 0)
    return lax.map(per_slot, (query_rows, key_rows, value_rows, cached_rows, active))
```

```python
import functools
import math

import jax
import jax.numpy as jnp
from jax import lax
from jax.experimental import pallas as pl
from jax.experimental.pallas import tpu as pltpu
from jax.sharding import PartitionSpec as P

HEAD_DIM = 128
MESH = pl.DeviceIdType.MESH
PARTS = 2
CUTS = 1
DELAY = 3
ORDER = ((1, 0), (2, 0), (1, 1), (2, 1), (0, 0), (0, 1))


def block_rows(row_count):
    for candidate in range(512, row_count + 1):
        if row_count % candidate == 0:
            return candidate
    return row_count


def attend(head_queries, head_keys, head_values):
    row_count, head_count, depth = head_queries.shape
    block = block_rows(row_count)
    factor = 1.0 / math.sqrt(depth)
    stacked = head_queries.reshape(row_count // block, block, head_count, depth)

    def one_block(query_block):
        scores = (
            jnp.einsum("qnd,knd->nqk", query_block, head_keys, preferred_element_type=jnp.float32)
            * factor
        )
        peak = jnp.max(scores, axis=2, keepdims=True)
        shifted = jnp.exp(scores - peak)
        total = jnp.sum(shifted, axis=2)
        weights = shifted.astype(jnp.bfloat16)
        mixed = jnp.einsum("nqk,knd->qnd", weights, head_values, preferred_element_type=jnp.float32)
        return (mixed / jnp.transpose(total)[:, :, None]).astype(jnp.bfloat16)

    return lax.map(one_block, stacked).reshape(row_count, head_count, depth)


def skipped(head_queries, head_keys, head_values):
    return jnp.zeros(head_queries.shape, jnp.bfloat16)


def plain_body(query_rows, key_rows, value_rows, cached_rows, plan, timestep, assignment):
    pieces = lax.axis_size("seq")
    local_rows = query_rows.shape[1]
    width = query_rows.shape[2]
    group = lax.axis_index("batch")
    slot_index = jnp.arange(assignment.shape[0], dtype=jnp.int32)
    request = jnp.sum(jnp.where(slot_index == group, assignment, 0))
    moment = jnp.sum(jnp.where(slot_index == request, timestep, 0))
    step_index = jnp.arange(plan.shape[1], dtype=jnp.int32)
    chosen = (slot_index[:, None] == request) & (step_index[None, :] == moment)
    active = jnp.sum(jnp.where(chosen, plan, 0)) > 0

    def arrange(rows):
        return rows[0].reshape(local_rows, pieces, width // (pieces * HEAD_DIM), HEAD_DIM)

    def gather(rows):
        return lax.all_to_all(arrange(rows), "seq", split_axis=1, concat_axis=0, tiled=True)[:, 0]

    attended = lax.cond(
        active, attend, skipped, gather(query_rows), gather(key_rows), gather(value_rows)
    )
    moved = lax.all_to_all(attended[:, None], "seq", split_axis=0, concat_axis=1, tiled=True)
    fresh = moved.reshape(1, local_rows, width)
    return jnp.where(active, fresh, cached_rows)


def exclusive(number, other, size):
    total = 0
    bit = 1
    while bit < size:
        total = total + bit * ((number // bit + other // bit) % 2)
        bit *= 2
    return total


def kernel(
    groups, pieces, stages,
    assignment_ref, timestep_ref, plan_ref, query_ref, key_ref, value_ref, cached_ref,
    out_ref,
    own, other, paired, gathered, mixed, backs, homes, cached,
    own_sem, other_sem, cached_sem, pair_send, pair_recv, ring_send, ring_recv,
    back_send, back_recv, home_send, home_recv,
):
    batch = lax.axis_index("batch")
    me = lax.axis_index("seq")
    half = groups // 2
    side = batch // half
    partner = (batch + half) % groups
    other_side = 1 - side
    rows = query_ref.shape[1]
    count = stages * pieces
    sources = (query_ref, key_ref, value_ref)

    request = assignment_ref[batch]
    moment = timestep_ref[request]
    active = plan_ref[request, moment] > 0

    def split(index):
        return index // pieces, pieces - 1 - index % pieces

    def columns(which, peer, stage):
        head = (which * pieces + peer) * stages + stage
        return pl.ds(pl.multiple_of(head * HEAD_DIM, HEAD_DIM), HEAD_DIM)

    def rows_of(peer):
        return pl.ds(pl.multiple_of(peer * rows, rows), rows)

    share = rows // PARTS
    slab = rows // CUTS

    def part_rows(part, peer=0):
        return pl.ds(pl.multiple_of(peer * rows + part * share, share), share)

    def cut_rows(cut, peer=0):
        return pl.ds(pl.multiple_of(peer * rows + cut * slab, slab), slab)

    def other_copy(index, kind):
        stage, offset = split(index)
        peer = exclusive(me, offset, pieces)
        return pltpu.make_async_copy(
            sources[kind].at[0, :, columns(other_side, peer, stage)],
            other.at[kind, index],
            other_sem.at[kind, index],
        )

    def pair_copy(index, kind, cut):
        return pltpu.make_async_remote_copy(
            src_ref=other.at[kind, index, cut_rows(cut)],
            dst_ref=paired.at[kind, index, cut_rows(cut)],
            send_sem=pair_send.at[kind, index, cut],
            recv_sem=pair_recv.at[kind, index, cut],
            device_id=(partner, me),
            device_id_type=MESH,
        )

    def ring_copy(index, kind, cut):
        stage, offset = split(index)
        peer = exclusive(me, offset, pieces)
        return pltpu.make_async_remote_copy(
            src_ref=paired.at[kind, index, cut_rows(cut)],
            dst_ref=gathered.at[kind, stage, cut_rows(cut, me)],
            send_sem=ring_send.at[kind, index, cut],
            recv_sem=ring_recv.at[kind, index, cut],
            device_id=(batch, peer),
            device_id_type=MESH,
        )

    def back_copy(index, part):
        stage, offset = split(index)
        peer = exclusive(me, offset, pieces)
        return pltpu.make_async_remote_copy(
            src_ref=mixed.at[stage, part_rows(part, peer)],
            dst_ref=backs.at[index, part_rows(part)],
            send_sem=back_send.at[index, part],
            recv_sem=back_recv.at[index, part],
            device_id=(batch, peer),
            device_id_type=MESH,
        )

    def home_copy(index, part):
        return pltpu.make_async_remote_copy(
            src_ref=backs.at[index, part_rows(part)],
            dst_ref=homes.at[index, part_rows(part)],
            send_sem=home_send.at[index, part],
            recv_sem=home_recv.at[index, part],
            device_id=(partner, me),
            device_id_type=MESH,
        )

    def settle(index, part, which, fresh):
        stage, offset = split(index)
        lanes = columns(which, exclusive(me, offset, pieces), stage)
        where = part_rows(part)
        out_ref[0, where, lanes] = lax.select_n(active, cached[where, lanes], fresh[index, where])

    def own_copy(kind):
        width = pieces * stages * HEAD_DIM
        start = pl.multiple_of(side * width, HEAD_DIM)
        return pltpu.make_async_copy(
            sources[kind].at[0, :, pl.ds(start, width)], own.at[kind], own_sem.at[kind]
        )

    barrier = pltpu.get_barrier_semaphore()
    pl.semaphore_signal(barrier, inc=1, device_id=(partner, me), device_id_type=MESH)
    for step in range(1, pieces):
        pl.semaphore_signal(
            barrier, inc=1, device_id=(batch, (me + step) % pieces), device_id_type=MESH
        )

    def load_others(group, carry):
        for kind, sub in ORDER:
            other_copy(2 * group + sub, kind).start()
        return carry

    lax.fori_loop(0, count // 2, load_others, 0)
    for kind in (1, 2, 0):
        own_copy(kind).start()
    pl.semaphore_wait(barrier, pieces)

    per_stage = 3 * pieces
    forwards = stages * per_stage
    stage_units = pieces * PARTS
    units = stages * stage_units
    start = per_stage + min(DELAY, 3 * pieces // 2)
    held_from = max(stages - 2, 0) * stage_units
    held_to = held_from + stage_units // 2 * (stages > 1)
    half_units = stage_units // 2
    lead = half_units // 2
    inner = (me + 1) // 2 % 2

    def start_pairs(group, carry):
        for kind, sub in ORDER:
            other_copy(2 * group + sub, kind).wait()
            for cut in range(CUTS):
                pair_copy(2 * group + sub, kind, cut).start()
        return carry

    start_pairs(0, 0)
    cached_copy = pltpu.make_async_copy(cached_ref.at[0], cached, cached_sem)
    cached_copy.start()
    for kind in range(3):
        own_copy(kind).wait()

    def forward(number):
        place = number % 6

        @pl.when((place == 0) & (number < forwards - 6))
        def _():
            start_pairs(number // 6 + 1, 0)

        late = place // 4
        kind = (1 - late) * (1 + place % 2)
        index = number // 6 * 2 + (1 - late) * (place // 2) + late * (place - 4)
        stage, offset = split(index)
        peer = exclusive(me, offset, pieces)
        lanes = pl.ds(pl.multiple_of((peer * stages + stage) * HEAD_DIM, HEAD_DIM), HEAD_DIM)
        for cut in range(CUTS):
            pair_copy(index, kind, cut).wait_recv()
            mine = own[kind, cut_rows(cut), lanes]
            chosen = lax.select_n(active, paired[kind, index, cut_rows(cut)], mine)

            @pl.when(offset != 0)
            def _():
                paired[kind, index, cut_rows(cut)] = chosen
                ring_copy(index, kind, cut).start()

            @pl.when(offset == 0)
            def _():
                gathered[kind, stage, cut_rows(cut, me), :] = chosen

    def send_back(unit, carry):
        index, part = unit // PARTS, unit % PARTS
        _, offset = split(index)

        @pl.when(offset != 0)
        def _():
            back_copy(index, part).start()

        return carry

    def unit_of(stage, place):
        crossing = place // half_units
        turned = (place + inner * (half_units // 2)) % half_units
        within = crossing * turned + (1 - crossing) * (half_units + place)
        unit = stage * stage_units + within
        return unit // PARTS, unit % PARTS

    def send_home(stage, place):
        index, part = unit_of(stage, place)
        _, offset = split(index)

        @pl.when(offset != 0)
        def _():
            back_copy(index, part).wait_recv()

        home_copy(index, part).start()
        settle(index, part, side, backs)

    def come_home(stage, place):
        index, part = unit_of(stage, place)
        home_copy(index, part).wait_recv()
        settle(index, part, other_side, homes)

    def each(first, number, low, high, action):
        span = high - low

        def body(item, carry):
            action(first + item // span, low + item % span)
            return carry

        lax.fori_loop(0, number * span, body, 0)

    def attention(unit, carry):
        index, part = unit // PARTS, unit % PARTS
        stage, offset = split(index)
        peer = exclusive(me, offset, pieces)

        @pl.when((unit % stage_units == 0) & (stage > 0))
        def _():
            each(stage - 1, 1, 0, half_units, send_home)

        @pl.when(unit % stage_units == 0)
        def _():
            def arrived(step, carry):
                for kind in (1, 2):
                    for cut in range(CUTS):
                        ring_copy(stage * pieces + step, kind, cut).wait_recv()
                return carry

            lax.fori_loop(0, pieces - 1, arrived, 0)

            @pl.when((unit == units - stage_units) & (inner == 0))
            def _():
                lax.fori_loop(held_from, held_to, send_back, 0)

        @pl.when((offset != 0) & (part == 0))
        def _():
            for cut in range(CUTS):
                ring_copy(index, 0, cut).wait_recv()

        factor = math.log2(math.e) / math.sqrt(HEAD_DIM)
        where = part_rows(part, peer)
        queries = gathered[0, stage, where, :]
        scores = lax.dot_general(
            queries, gathered[1, stage], (((1,), (1,)), ((), ())),
            preferred_element_type=jnp.float32,
        )
        peak = jnp.max(scores, axis=1, keepdims=True)
        weights = jnp.exp2((scores - peak) * factor)
        total = jnp.sum(weights, axis=1, keepdims=True)
        result = jnp.dot(
            weights.astype(jnp.bfloat16), gathered[2, stage], preferred_element_type=jnp.float32
        )
        blended = (result / total).astype(jnp.bfloat16)

        @pl.when(offset != 0)
        def _():
            mixed[stage, where, :] = blended

        @pl.when(offset == 0)
        def _():
            backs[index, part_rows(part)] = blended

        @pl.when((unit < held_from) | (unit >= held_to))
        def _():
            send_back(unit, 0)

        spot = unit % stage_units

        @pl.when((stage > 0) & (spot >= half_units) & (unit < units - lead))
        def _():
            send_home(stage - 1, spot)

        return carry

    def early(number, carry):
        forward(number)
        return carry

    lax.fori_loop(0, min(start, forwards), early, 0)
    cached_copy.wait()

    def step_of(number, carry):
        @pl.when(number < forwards)
        def _():
            forward(number)

        done = number - start
        lax.fori_loop(done * PARTS // 3, (done + 1) * PARTS // 3, attention, 0)

        @pl.when((number == forwards - 1) & (inner == 1))
        def _():
            lax.fori_loop(held_from, held_to, send_back, 0)

        return carry

    lax.fori_loop(start, start + forwards, step_of, 0)
    def inputs_sent(index, carry):
        _, offset = split(index)
        for kind in range(3):
            for cut in range(CUTS):
                pair_copy(index, kind, cut).wait_send()

        @pl.when(offset != 0)
        def _():
            for kind in range(3):
                for cut in range(CUTS):
                    ring_copy(index, kind, cut).wait_send()

        return carry

    def outputs_sent(index, carry):
        _, offset = split(index)
        for part in range(PARTS):
            home_copy(index, part).wait_send()

        @pl.when(offset != 0)
        def _():
            for part in range(PARTS):
                back_copy(index, part).wait_send()

        return carry

    outer = half_units + lead
    final = stages - 1
    few = max(final - 1, 0)
    each(final, 1, 0, half_units, send_home)
    each(final, 1, half_units, outer, send_home)
    lax.fori_loop(0, count, inputs_sent, 0)
    each(0, few, 0, stage_units, come_home)
    each(few, final - few, 0, outer, come_home)
    each(few, final - few, outer, stage_units, send_home)
    each(final, 1, 0, half_units, come_home)
    each(final, 1, outer, stage_units, send_home)
    each(final, 1, half_units, outer, come_home)
    each(few, stages - few, outer, stage_units, come_home)
    lax.fori_loop(0, count, outputs_sent, 0)


def paired_body(query_rows, key_rows, value_rows, cached_rows, plan, timestep, assignment):
    groups = lax.axis_size("batch")
    pieces = lax.axis_size("seq")
    _, rows, width = query_rows.shape
    stages = width // HEAD_DIM // (2 * pieces)
    count = stages * pieces
    smem = pl.BlockSpec(memory_space=pltpu.SMEM)
    anywhere = pl.BlockSpec(memory_space=pl.ANY)
    block = (rows, HEAD_DIM)
    return pl.pallas_call(
        functools.partial(kernel, groups, pieces, stages),
        out_shape=pltpu.VMEM(query_rows.shape, jnp.bfloat16),
        in_specs=[smem] * 3 + [anywhere] * 4,
        out_specs=pl.BlockSpec(memory_space=pltpu.VMEM),
        scratch_shapes=[
            pltpu.VMEM((3, rows, width // 2), jnp.bfloat16),
            pltpu.VMEM((3, count) + block, jnp.bfloat16),
            pltpu.VMEM((3, count) + block, jnp.bfloat16),
            pltpu.VMEM((3, stages, pieces * rows, HEAD_DIM), jnp.bfloat16),
            pltpu.VMEM((stages, pieces * rows, HEAD_DIM), jnp.bfloat16),
            pltpu.VMEM((count,) + block, jnp.bfloat16),
            pltpu.VMEM((count,) + block, jnp.bfloat16),
            pltpu.VMEM((rows, width), jnp.bfloat16),
            pltpu.SemaphoreType.DMA((3,)),
            pltpu.SemaphoreType.DMA((3, count)),
            pltpu.SemaphoreType.DMA,
            pltpu.SemaphoreType.DMA((3, count, CUTS)),
            pltpu.SemaphoreType.DMA((3, count, CUTS)),
            pltpu.SemaphoreType.DMA((3, count, CUTS)),
            pltpu.SemaphoreType.DMA((3, count, CUTS)),
            pltpu.SemaphoreType.DMA((count, PARTS)),
            pltpu.SemaphoreType.DMA((count, PARTS)),
            pltpu.SemaphoreType.DMA((count, PARTS)),
            pltpu.SemaphoreType.DMA((count, PARTS)),
        ],
        compiler_params=pltpu.CompilerParams(
            collective_id=0, has_side_effects=True, vmem_limit_bytes=56 << 20
        ),
    )(assignment, timestep, plan, query_rows, key_rows, value_rows, cached_rows)


def solution(mesh):
    placed = (
        P("batch", "seq", None),
        P("batch", "seq", None),
        P("batch", "seq", None),
        P("batch", "seq", None),
        P(),
        P(),
        P(),
    )
    groups, pieces = mesh.shape["batch"], mesh.shape["seq"]

    def body(query_rows, *rest):
        heads = query_rows.shape[2] // HEAD_DIM
        rows = query_rows.shape[1]
        even = groups % 2 == 0 and heads % (2 * pieces) == 0 and rows % (16 * PARTS * CUTS) == 0
        power = pieces > 1 and pieces & (pieces - 1) == 0
        chosen = paired_body if even and power else plain_body
        return chosen(query_rows, *rest)

    return jax.shard_map(
        body, mesh=mesh, in_specs=placed, out_specs=P("batch", "seq", None), check_vma=False
    )
```

```python
import functools
import math

import jax
import jax.numpy as jnp
from jax import lax
from jax.experimental import pallas as pl
from jax.experimental.pallas import tpu as pltpu
from jax.sharding import PartitionSpec as P

HEAD_DIM = 128
MESH = pl.DeviceIdType.MESH
PARTS = 2
CUTS = 1
DELAY = 3
ORDER = ((1, 0), (2, 0), (1, 1), (2, 1), (0, 0), (0, 1))


def block_rows(row_count):
    for candidate in range(512, row_count + 1):
        if row_count % candidate == 0:
            return candidate
    return row_count


def attend(head_queries, head_keys, head_values):
    row_count, head_count, depth = head_queries.shape
    block = block_rows(row_count)
    factor = 1.0 / math.sqrt(depth)
    stacked = head_queries.reshape(row_count // block, block, head_count, depth)

    def one_block(query_block):
        scores = (
            jnp.einsum("qnd,knd->nqk", query_block, head_keys, preferred_element_type=jnp.float32)
            * factor
        )
        peak = jnp.max(scores, axis=2, keepdims=True)
        shifted = jnp.exp(scores - peak)
        total = jnp.sum(shifted, axis=2)
        weights = shifted.astype(jnp.bfloat16)
        mixed = jnp.einsum("nqk,knd->qnd", weights, head_values, preferred_element_type=jnp.float32)
        return (mixed / jnp.transpose(total)[:, :, None]).astype(jnp.bfloat16)

    return lax.map(one_block, stacked).reshape(row_count, head_count, depth)


def skipped(head_queries, head_keys, head_values):
    return jnp.zeros(head_queries.shape, jnp.bfloat16)


def plain_body(query_rows, key_rows, value_rows, cached_rows, plan, timestep, assignment):
    pieces = lax.axis_size("seq")
    local_rows = query_rows.shape[1]
    width = query_rows.shape[2]
    group = lax.axis_index("batch")
    slot_index = jnp.arange(assignment.shape[0], dtype=jnp.int32)
    request = jnp.sum(jnp.where(slot_index == group, assignment, 0))
    moment = jnp.sum(jnp.where(slot_index == request, timestep, 0))
    step_index = jnp.arange(plan.shape[1], dtype=jnp.int32)
    chosen = (slot_index[:, None] == request) & (step_index[None, :] == moment)
    active = jnp.sum(jnp.where(chosen, plan, 0)) > 0

    def arrange(rows):
        return rows[0].reshape(local_rows, pieces, width // (pieces * HEAD_DIM), HEAD_DIM)

    def gather(rows):
        return lax.all_to_all(arrange(rows), "seq", split_axis=1, concat_axis=0, tiled=True)[:, 0]

    attended = lax.cond(
        active, attend, skipped, gather(query_rows), gather(key_rows), gather(value_rows)
    )
    moved = lax.all_to_all(attended[:, None], "seq", split_axis=0, concat_axis=1, tiled=True)
    fresh = moved.reshape(1, local_rows, width)
    return jnp.where(active, fresh, cached_rows)


def exclusive(number, other, size):
    total = 0
    bit = 1
    while bit < size:
        total = total + bit * ((number // bit + other // bit) % 2)
        bit *= 2
    return total


def kernel(
    groups, pieces, stages,
    assignment_ref, timestep_ref, plan_ref, query_ref, key_ref, value_ref, cached_ref,
    out_ref,
    own, other, paired, gathered, mixed, backs, homes, cached,
    own_sem, other_sem, cached_sem, pair_send, pair_recv, ring_send, ring_recv,
    back_send, back_recv, home_send, home_recv,
):
    batch = lax.axis_index("batch")
    me = lax.axis_index("seq")
    half = groups // 2
    side = batch // half
    partner = (batch + half) % groups
    other_side = 1 - side
    rows = query_ref.shape[1]
    count = stages * pieces
    sources = (query_ref, key_ref, value_ref)

    request = assignment_ref[batch]
    moment = timestep_ref[request]
    active = plan_ref[request, moment] > 0

    def split(index):
        return index // pieces, pieces - 1 - index % pieces

    def columns(which, peer, stage):
        head = (which * pieces + peer) * stages + stage
        return pl.ds(pl.multiple_of(head * HEAD_DIM, HEAD_DIM), HEAD_DIM)

    def rows_of(peer):
        return pl.ds(pl.multiple_of(peer * rows, rows), rows)

    share = rows // PARTS
    slab = rows // CUTS

    def part_rows(part, peer=0):
        return pl.ds(pl.multiple_of(peer * rows + part * share, share), share)

    def cut_rows(cut, peer=0):
        return pl.ds(pl.multiple_of(peer * rows + cut * slab, slab), slab)

    def other_copy(index, kind):
        stage, offset = split(index)
        peer = exclusive(me, offset, pieces)
        return pltpu.make_async_copy(
            sources[kind].at[0, :, columns(other_side, peer, stage)],
            other.at[kind, index],
            other_sem.at[kind, index],
        )

    def pair_copy(index, kind, cut):
        return pltpu.make_async_remote_copy(
            src_ref=other.at[kind, index, cut_rows(cut)],
            dst_ref=paired.at[kind, index, cut_rows(cut)],
            send_sem=pair_send.at[kind, index, cut],
            recv_sem=pair_recv.at[kind, index, cut],
            device_id=(partner, me),
            device_id_type=MESH,
        )

    def ring_copy(index, kind, cut):
        stage, offset = split(index)
        peer = exclusive(me, offset, pieces)
        return pltpu.make_async_remote_copy(
            src_ref=paired.at[kind, index, cut_rows(cut)],
            dst_ref=gathered.at[kind, stage, cut_rows(cut, me)],
            send_sem=ring_send.at[kind, index, cut],
            recv_sem=ring_recv.at[kind, index, cut],
            device_id=(batch, peer),
            device_id_type=MESH,
        )

    def back_copy(index, part):
        stage, offset = split(index)
        peer = exclusive(me, offset, pieces)
        return pltpu.make_async_remote_copy(
            src_ref=mixed.at[stage, part_rows(part, peer)],
            dst_ref=backs.at[index, part_rows(part)],
            send_sem=back_send.at[index, part],
            recv_sem=back_recv.at[index, part],
            device_id=(batch, peer),
            device_id_type=MESH,
        )

    def home_copy(index, part):
        return pltpu.make_async_remote_copy(
            src_ref=backs.at[index, part_rows(part)],
            dst_ref=homes.at[index, part_rows(part)],
            send_sem=home_send.at[index, part],
            recv_sem=home_recv.at[index, part],
            device_id=(partner, me),
            device_id_type=MESH,
        )

    def settle(index, part, which, fresh):
        stage, offset = split(index)
        lanes = columns(which, exclusive(me, offset, pieces), stage)
        where = part_rows(part)
        out_ref[0, where, lanes] = lax.select_n(active, cached[where, lanes], fresh[index, where])

    def own_copy(kind):
        width = pieces * stages * HEAD_DIM
        start = pl.multiple_of(side * width, HEAD_DIM)
        return pltpu.make_async_copy(
            sources[kind].at[0, :, pl.ds(start, width)], own.at[kind], own_sem.at[kind]
        )

    barrier = pltpu.get_barrier_semaphore()
    pl.semaphore_signal(barrier, inc=1, device_id=(partner, me), device_id_type=MESH)
    for step in range(1, pieces):
        pl.semaphore_signal(
            barrier, inc=1, device_id=(batch, (me + step) % pieces), device_id_type=MESH
        )

    def load_others(group, carry):
        for kind, sub in ORDER:
            other_copy(2 * group + sub, kind).start()
        return carry

    lax.fori_loop(0, count // 2, load_others, 0)
    for kind in (1, 2, 0):
        own_copy(kind).start()
    pl.semaphore_wait(barrier, pieces)

    per_stage = 3 * pieces
    forwards = stages * per_stage
    stage_units = pieces * PARTS
    units = stages * stage_units
    start = per_stage + min(DELAY, 3 * (pieces // 2 - 1))
    held_from = max(stages - 2, 0) * stage_units
    held_to = held_from + stage_units // 2 * (stages > 1)
    half_units = stage_units // 2
    lead = half_units // 2
    inner = (me + 1) // 2 % 2

    def start_pairs(group, carry):
        for kind, sub in ORDER:
            other_copy(2 * group + sub, kind).wait()
            for cut in range(CUTS):
                pair_copy(2 * group + sub, kind, cut).start()
        return carry

    start_pairs(0, 0)
    cached_copy = pltpu.make_async_copy(cached_ref.at[0], cached, cached_sem)
    cached_copy.start()
    for kind in range(3):
        own_copy(kind).wait()

    def forward(number):
        place = number % 6

        @pl.when((place == 0) & (number < forwards - 6))
        def _():
            start_pairs(number // 6 + 1, 0)

        late = place // 4
        kind = (1 - late) * (1 + place % 2)
        index = number // 6 * 2 + (1 - late) * (place // 2) + late * (place - 4)
        stage, offset = split(index)
        peer = exclusive(me, offset, pieces)
        lanes = pl.ds(pl.multiple_of((peer * stages + stage) * HEAD_DIM, HEAD_DIM), HEAD_DIM)
        for cut in range(CUTS):
            pair_copy(index, kind, cut).wait_recv()
            mine = own[kind, cut_rows(cut), lanes]
            chosen = lax.select_n(active, paired[kind, index, cut_rows(cut)], mine)

            @pl.when(offset != 0)
            def _():
                paired[kind, index, cut_rows(cut)] = chosen
                ring_copy(index, kind, cut).start()

            @pl.when(offset == 0)
            def _():
                gathered[kind, stage, cut_rows(cut, me), :] = chosen

    def send_back(unit, carry):
        index, part = unit // PARTS, unit % PARTS
        _, offset = split(index)

        @pl.when(offset != 0)
        def _():
            back_copy(index, part).start()

        return carry

    def unit_of(stage, place):
        crossing = place // half_units
        turned = (place + inner * (half_units // 2)) % half_units
        within = crossing * turned + (1 - crossing) * (half_units + place)
        unit = stage * stage_units + within
        return unit // PARTS, unit % PARTS

    def send_home(stage, place):
        index, part = unit_of(stage, place)
        _, offset = split(index)

        @pl.when(offset != 0)
        def _():
            back_copy(index, part).wait_recv()

        home_copy(index, part).start()
        settle(index, part, side, backs)

    def come_home(stage, place):
        index, part = unit_of(stage, place)
        home_copy(index, part).wait_recv()
        settle(index, part, other_side, homes)

    def each(first, number, low, high, action):
        span = high - low

        def body(item, carry):
            action(first + item // span, low + item % span)
            return carry

        lax.fori_loop(0, number * span, body, 0)

    def attention(unit, carry):
        turn, part = unit // PARTS, unit % PARTS
        index = turn // pieces * pieces + (turn + pieces - 1) % pieces
        stage, offset = split(index)
        peer = exclusive(me, offset, pieces)

        @pl.when((unit % stage_units == 0) & (stage > 0))
        def _():
            each(stage - 1, 1, 0, half_units - PARTS, send_home)

        @pl.when(unit % stage_units == 0)
        def _():
            def arrived(step, carry):
                for kind in (1, 2):
                    for cut in range(CUTS):
                        ring_copy(stage * pieces + step, kind, cut).wait_recv()
                return carry

            lax.fori_loop(0, pieces - 1, arrived, 0)

            @pl.when((unit == units - stage_units) & (inner == 0))
            def _():
                lax.fori_loop(held_from, held_to, send_back, 0)

        @pl.when((offset != 0) & (part == 0))
        def _():
            for cut in range(CUTS):
                ring_copy(index, 0, cut).wait_recv()

        factor = math.log2(math.e) / math.sqrt(HEAD_DIM)
        where = part_rows(part, peer)
        queries = gathered[0, stage, where, :]
        scores = lax.dot_general(
            queries, gathered[1, stage], (((1,), (1,)), ((), ())),
            preferred_element_type=jnp.float32,
        )
        peak = jnp.max(scores, axis=1, keepdims=True)
        weights = jnp.exp2((scores - peak) * factor)
        total = jnp.sum(weights, axis=1, keepdims=True)
        result = jnp.dot(
            weights.astype(jnp.bfloat16), gathered[2, stage], preferred_element_type=jnp.float32
        )
        blended = (result / total).astype(jnp.bfloat16)

        @pl.when(offset != 0)
        def _():
            mixed[stage, where, :] = blended

        @pl.when(offset == 0)
        def _():
            backs[index, part_rows(part)] = blended
            home_copy(index, part).start()
            settle(index, part, side, backs)

        @pl.when((stage != stages - 2) | (offset < pieces // 2))
        def _():
            send_back(index * PARTS + part, 0)

        spot = unit % stage_units

        @pl.when((stage > 0) & (spot >= half_units) & (unit < units - lead))
        def _():
            send_home(stage - 1, spot)

        @pl.when(unit >= units - lead)
        def _():
            send_home(stage, spot - lead)

        return carry

    def early(number, carry):
        forward(number)
        return carry

    lax.fori_loop(0, min(start, forwards), early, 0)
    cached_copy.wait()

    def step_of(number, carry):
        @pl.when(number < forwards)
        def _():
            forward(number)

        done = number - start
        lax.fori_loop(done * PARTS // 3, (done + 1) * PARTS // 3, attention, 0)

        @pl.when((number == forwards - 1) & (inner == 1))
        def _():
            lax.fori_loop(held_from, held_to, send_back, 0)

        return carry

    lax.fori_loop(start, start + forwards, step_of, 0)
    def inputs_sent(index, carry):
        _, offset = split(index)
        for kind in range(3):
            for cut in range(CUTS):
                pair_copy(index, kind, cut).wait_send()

        @pl.when(offset != 0)
        def _():
            for kind in range(3):
                for cut in range(CUTS):
                    ring_copy(index, kind, cut).wait_send()

        return carry

    def outputs_sent(index, carry):
        _, offset = split(index)
        for part in range(PARTS):
            home_copy(index, part).wait_send()

        @pl.when(offset != 0)
        def _():
            for part in range(PARTS):
                back_copy(index, part).wait_send()

        return carry

    outer = half_units + lead
    final = stages - 1
    few = max(final - 1, 0)
    each(final, 1, 0, half_units - PARTS, send_home)
    lax.fori_loop(0, count, inputs_sent, 0)
    each(0, few, 0, stage_units, come_home)
    each(few, final - few, 0, outer, come_home)
    each(few, final - few, outer, stage_units, send_home)
    each(final, 1, half_units - PARTS, outer, come_home)
    each(final, 1, outer, stage_units, send_home)
    each(final, 1, 0, half_units - PARTS, come_home)
    each(few, stages - few, outer, stage_units, come_home)
    lax.fori_loop(0, count, outputs_sent, 0)


def paired_body(query_rows, key_rows, value_rows, cached_rows, plan, timestep, assignment):
    groups = lax.axis_size("batch")
    pieces = lax.axis_size("seq")
    _, rows, width = query_rows.shape
    stages = width // HEAD_DIM // (2 * pieces)
    count = stages * pieces
    smem = pl.BlockSpec(memory_space=pltpu.SMEM)
    anywhere = pl.BlockSpec(memory_space=pl.ANY)
    block = (rows, HEAD_DIM)
    return pl.pallas_call(
        functools.partial(kernel, groups, pieces, stages),
        out_shape=pltpu.VMEM(query_rows.shape, jnp.bfloat16),
        in_specs=[smem] * 3 + [anywhere] * 4,
        out_specs=pl.BlockSpec(memory_space=pltpu.VMEM),
        scratch_shapes=[
            pltpu.VMEM((3, rows, width // 2), jnp.bfloat16),
            pltpu.VMEM((3, count) + block, jnp.bfloat16),
            pltpu.VMEM((3, count) + block, jnp.bfloat16),
            pltpu.VMEM((3, stages, pieces * rows, HEAD_DIM), jnp.bfloat16),
            pltpu.VMEM((stages, pieces * rows, HEAD_DIM), jnp.bfloat16),
            pltpu.VMEM((count,) + block, jnp.bfloat16),
            pltpu.VMEM((count,) + block, jnp.bfloat16),
            pltpu.VMEM((rows, width), jnp.bfloat16),
            pltpu.SemaphoreType.DMA((3,)),
            pltpu.SemaphoreType.DMA((3, count)),
            pltpu.SemaphoreType.DMA,
            pltpu.SemaphoreType.DMA((3, count, CUTS)),
            pltpu.SemaphoreType.DMA((3, count, CUTS)),
            pltpu.SemaphoreType.DMA((3, count, CUTS)),
            pltpu.SemaphoreType.DMA((3, count, CUTS)),
            pltpu.SemaphoreType.DMA((count, PARTS)),
            pltpu.SemaphoreType.DMA((count, PARTS)),
            pltpu.SemaphoreType.DMA((count, PARTS)),
            pltpu.SemaphoreType.DMA((count, PARTS)),
        ],
        compiler_params=pltpu.CompilerParams(
            collective_id=0, has_side_effects=True, vmem_limit_bytes=56 << 20
        ),
    )(assignment, timestep, plan, query_rows, key_rows, value_rows, cached_rows)


def solution(mesh):
    placed = (
        P("batch", "seq", None),
        P("batch", "seq", None),
        P("batch", "seq", None),
        P("batch", "seq", None),
        P(),
        P(),
        P(),
    )
    groups, pieces = mesh.shape["batch"], mesh.shape["seq"]

    def body(query_rows, *rest):
        heads = query_rows.shape[2] // HEAD_DIM
        rows = query_rows.shape[1]
        even = groups % 2 == 0 and heads % (2 * pieces) == 0 and rows % (16 * PARTS * CUTS) == 0
        power = pieces > 1 and pieces & (pieces - 1) == 0
        chosen = paired_body if even and power else plain_body
        return chosen(query_rows, *rest)

    return jax.shard_map(
        body, mesh=mesh, in_specs=placed, out_specs=P("batch", "seq", None), check_vma=False
    )
```

```python
import functools
import math

import jax
import jax.numpy as jnp
from jax import lax
from jax.experimental import pallas as pl
from jax.experimental.pallas import tpu as pltpu
from jax.sharding import PartitionSpec as P

HEAD_DIM = 128
MESH = pl.DeviceIdType.MESH
PARTS = 4
CUTS = 1
DELAY = 3
ORDER = ((1, 0), (2, 0), (1, 1), (2, 1), (0, 0), (0, 1))


def block_rows(row_count):
    for candidate in range(512, row_count + 1):
        if row_count % candidate == 0:
            return candidate
    return row_count


def attend(head_queries, head_keys, head_values):
    row_count, head_count, depth = head_queries.shape
    block = block_rows(row_count)
    factor = 1.0 / math.sqrt(depth)
    stacked = head_queries.reshape(row_count // block, block, head_count, depth)

    def one_block(query_block):
        scores = (
            jnp.einsum("qnd,knd->nqk", query_block, head_keys, preferred_element_type=jnp.float32)
            * factor
        )
        peak = jnp.max(scores, axis=2, keepdims=True)
        shifted = jnp.exp(scores - peak)
        total = jnp.sum(shifted, axis=2)
        weights = shifted.astype(jnp.bfloat16)
        mixed = jnp.einsum("nqk,knd->qnd", weights, head_values, preferred_element_type=jnp.float32)
        return (mixed / jnp.transpose(total)[:, :, None]).astype(jnp.bfloat16)

    return lax.map(one_block, stacked).reshape(row_count, head_count, depth)


def skipped(head_queries, head_keys, head_values):
    return jnp.zeros(head_queries.shape, jnp.bfloat16)


def plain_body(query_rows, key_rows, value_rows, cached_rows, plan, timestep, assignment):
    pieces = lax.axis_size("seq")
    local_rows = query_rows.shape[1]
    width = query_rows.shape[2]
    group = lax.axis_index("batch")
    slot_index = jnp.arange(assignment.shape[0], dtype=jnp.int32)
    request = jnp.sum(jnp.where(slot_index == group, assignment, 0))
    moment = jnp.sum(jnp.where(slot_index == request, timestep, 0))
    step_index = jnp.arange(plan.shape[1], dtype=jnp.int32)
    chosen = (slot_index[:, None] == request) & (step_index[None, :] == moment)
    active = jnp.sum(jnp.where(chosen, plan, 0)) > 0

    def arrange(rows):
        return rows[0].reshape(local_rows, pieces, width // (pieces * HEAD_DIM), HEAD_DIM)

    def gather(rows):
        return lax.all_to_all(arrange(rows), "seq", split_axis=1, concat_axis=0, tiled=True)[:, 0]

    attended = lax.cond(
        active, attend, skipped, gather(query_rows), gather(key_rows), gather(value_rows)
    )
    moved = lax.all_to_all(attended[:, None], "seq", split_axis=0, concat_axis=1, tiled=True)
    fresh = moved.reshape(1, local_rows, width)
    return jnp.where(active, fresh, cached_rows)


def exclusive(number, other, size):
    total = 0
    bit = 1
    while bit < size:
        total = total + bit * ((number // bit + other // bit) % 2)
        bit *= 2
    return total


def kernel(
    groups, pieces, stages,
    assignment_ref, timestep_ref, plan_ref, query_ref, key_ref, value_ref, cached_ref,
    out_ref,
    own, other, paired, gathered, mixed, backs, homes, cached,
    own_sem, other_sem, cached_sem, pair_send, pair_recv, ring_send, ring_recv,
    back_send, back_recv, home_send, home_recv,
):
    batch = lax.axis_index("batch")
    me = lax.axis_index("seq")
    half = groups // 2
    side = batch // half
    partner = (batch + half) % groups
    other_side = 1 - side
    rows = query_ref.shape[1]
    count = stages * pieces
    sources = (query_ref, key_ref, value_ref)

    request = assignment_ref[batch]
    moment = timestep_ref[request]
    active = plan_ref[request, moment] > 0

    def split(index):
        return index // pieces, pieces - 1 - index % pieces

    def columns(which, peer, stage):
        head = (which * pieces + peer) * stages + stage
        return pl.ds(pl.multiple_of(head * HEAD_DIM, HEAD_DIM), HEAD_DIM)

    def rows_of(peer):
        return pl.ds(pl.multiple_of(peer * rows, rows), rows)

    share = rows // PARTS
    slab = rows // CUTS

    def part_rows(part, peer=0):
        return pl.ds(pl.multiple_of(peer * rows + part * share, share), share)

    def cut_rows(cut, peer=0):
        return pl.ds(pl.multiple_of(peer * rows + cut * slab, slab), slab)

    def other_copy(index, kind):
        stage, offset = split(index)
        peer = exclusive(me, offset, pieces)
        return pltpu.make_async_copy(
            sources[kind].at[0, :, columns(other_side, peer, stage)],
            other.at[kind, index],
            other_sem.at[kind, index],
        )

    def pair_copy(index, kind, cut):
        return pltpu.make_async_remote_copy(
            src_ref=other.at[kind, index, cut_rows(cut)],
            dst_ref=paired.at[kind, index, cut_rows(cut)],
            send_sem=pair_send.at[kind, index, cut],
            recv_sem=pair_recv.at[kind, index, cut],
            device_id=(partner, me),
            device_id_type=MESH,
        )

    def ring_copy(index, kind, cut):
        stage, offset = split(index)
        peer = exclusive(me, offset, pieces)
        return pltpu.make_async_remote_copy(
            src_ref=paired.at[kind, index, cut_rows(cut)],
            dst_ref=gathered.at[kind, stage, cut_rows(cut, me)],
            send_sem=ring_send.at[kind, index, cut],
            recv_sem=ring_recv.at[kind, index, cut],
            device_id=(batch, peer),
            device_id_type=MESH,
        )

    def back_copy(index, part):
        stage, offset = split(index)
        peer = exclusive(me, offset, pieces)
        return pltpu.make_async_remote_copy(
            src_ref=mixed.at[stage, part_rows(part, peer)],
            dst_ref=backs.at[index, part_rows(part)],
            send_sem=back_send.at[index, part],
            recv_sem=back_recv.at[index, part],
            device_id=(batch, peer),
            device_id_type=MESH,
        )

    def home_copy(index, part):
        return pltpu.make_async_remote_copy(
            src_ref=backs.at[index, part_rows(part)],
            dst_ref=homes.at[index, part_rows(part)],
            send_sem=home_send.at[index, part],
            recv_sem=home_recv.at[index, part],
            device_id=(partner, me),
            device_id_type=MESH,
        )

    def settle(index, part, which, fresh):
        stage, offset = split(index)
        lanes = columns(which, exclusive(me, offset, pieces), stage)
        where = part_rows(part)
        out_ref[0, where, lanes] = lax.select_n(active, cached[where, lanes], fresh[index, where])

    def own_copy(kind):
        width = pieces * stages * HEAD_DIM
        start = pl.multiple_of(side * width, HEAD_DIM)
        return pltpu.make_async_copy(
            sources[kind].at[0, :, pl.ds(start, width)], own.at[kind], own_sem.at[kind]
        )

    barrier = pltpu.get_barrier_semaphore()
    pl.semaphore_signal(barrier, inc=1, device_id=(partner, me), device_id_type=MESH)
    for step in range(1, pieces):
        pl.semaphore_signal(
            barrier, inc=1, device_id=(batch, (me + step) % pieces), device_id_type=MESH
        )

    def load_others(group, carry):
        for kind, sub in ORDER:
            other_copy(2 * group + sub, kind).start()
        return carry

    lax.fori_loop(0, count // 2, load_others, 0)
    for kind in (1, 2, 0):
        own_copy(kind).start()
    pl.semaphore_wait(barrier, pieces)

    per_stage = 3 * pieces
    forwards = stages * per_stage
    stage_units = pieces * PARTS
    units = stages * stage_units
    start = per_stage + min(DELAY, 3 * (pieces // 2 - 1))
    held_from = max(stages - 2, 0) * stage_units
    held_to = held_from + stage_units // 2 * (stages > 1)
    half_units = stage_units // 2
    lead = half_units // 2
    inner = (me + 1) // 2 % 2

    def start_pairs(group, carry):
        for kind, sub in ORDER:
            other_copy(2 * group + sub, kind).wait()
            for cut in range(CUTS):
                pair_copy(2 * group + sub, kind, cut).start()
        return carry

    start_pairs(0, 0)
    cached_copy = pltpu.make_async_copy(cached_ref.at[0], cached, cached_sem)
    cached_copy.start()
    for kind in range(3):
        own_copy(kind).wait()

    def forward(number):
        place = number % 6

        @pl.when((place == 0) & (number < forwards - 6))
        def _():
            start_pairs(number // 6 + 1, 0)

        late = place // 4
        kind = (1 - late) * (1 + place % 2)
        index = number // 6 * 2 + (1 - late) * (place // 2) + late * (place - 4)
        stage, offset = split(index)
        peer = exclusive(me, offset, pieces)
        lanes = pl.ds(pl.multiple_of((peer * stages + stage) * HEAD_DIM, HEAD_DIM), HEAD_DIM)
        for cut in range(CUTS):
            pair_copy(index, kind, cut).wait_recv()
            mine = own[kind, cut_rows(cut), lanes]
            chosen = lax.select_n(active, paired[kind, index, cut_rows(cut)], mine)

            @pl.when(offset != 0)
            def _():
                paired[kind, index, cut_rows(cut)] = chosen
                ring_copy(index, kind, cut).start()

            @pl.when(offset == 0)
            def _():
                gathered[kind, stage, cut_rows(cut, me), :] = chosen

    def send_back(unit, carry):
        index, part = unit // PARTS, unit % PARTS
        _, offset = split(index)

        @pl.when(offset != 0)
        def _():
            back_copy(index, part).start()

        return carry

    def unit_of(stage, place):
        crossing = place // half_units
        turned = (place + inner * (half_units // 2)) % half_units
        within = crossing * turned + (1 - crossing) * (half_units + place)
        unit = stage * stage_units + within
        return unit // PARTS, unit % PARTS

    def send_home(stage, place):
        index, part = unit_of(stage, place)
        _, offset = split(index)

        @pl.when(offset != 0)
        def _():
            back_copy(index, part).wait_recv()

        home_copy(index, part).start()
        settle(index, part, side, backs)

    def come_home(stage, place):
        index, part = unit_of(stage, place)
        home_copy(index, part).wait_recv()
        settle(index, part, other_side, homes)

    def each(first, number, low, high, action):
        span = high - low

        def body(item, carry):
            action(first + item // span, low + item % span)
            return carry

        lax.fori_loop(0, number * span, body, 0)

    def attention(unit, carry):
        turn, part = unit // PARTS, unit % PARTS
        index = turn // pieces * pieces + (turn + pieces - 1) % pieces
        stage, offset = split(index)
        peer = exclusive(me, offset, pieces)

        @pl.when((unit % stage_units == 0) & (stage > 0))
        def _():
            each(stage - 1, 1, 0, half_units - PARTS, send_home)

        @pl.when(unit % stage_units == 0)
        def _():
            def arrived(step, carry):
                for kind in (1, 2):
                    for cut in range(CUTS):
                        ring_copy(stage * pieces + step, kind, cut).wait_recv()
                return carry

            lax.fori_loop(0, pieces - 1, arrived, 0)

            @pl.when((unit == units - stage_units) & (inner == 0))
            def _():
                lax.fori_loop(held_from, held_to, send_back, 0)

        @pl.when((offset != 0) & (part == 0))
        def _():
            for cut in range(CUTS):
                ring_copy(index, 0, cut).wait_recv()

        factor = math.log2(math.e) / math.sqrt(HEAD_DIM)
        where = part_rows(part, peer)
        queries = gathered[0, stage, where, :]
        scores = lax.dot_general(
            queries, gathered[1, stage], (((1,), (1,)), ((), ())),
            preferred_element_type=jnp.float32,
        )
        peak = jnp.max(scores, axis=1, keepdims=True)
        weights = jnp.exp2((scores - peak) * factor)
        total = jnp.sum(weights, axis=1, keepdims=True)
        result = jnp.dot(
            weights.astype(jnp.bfloat16), gathered[2, stage], preferred_element_type=jnp.float32
        )
        blended = (result / total).astype(jnp.bfloat16)

        @pl.when(offset != 0)
        def _():
            mixed[stage, where, :] = blended

        @pl.when(offset == 0)
        def _():
            backs[index, part_rows(part)] = blended
            home_copy(index, part).start()
            settle(index, part, side, backs)

        @pl.when((stage != stages - 2) | (offset < pieces // 2))
        def _():
            send_back(index * PARTS + part, 0)

        spot = unit % stage_units

        @pl.when((stage > 0) & (spot >= half_units) & (unit < units - lead))
        def _():
            send_home(stage - 1, spot)

        @pl.when(unit >= units - lead)
        def _():
            send_home(stage, spot - lead)

        return carry

    def early(number, carry):
        forward(number)
        return carry

    lax.fori_loop(0, min(start, forwards), early, 0)
    cached_copy.wait()

    def step_of(number, carry):
        @pl.when(number < forwards)
        def _():
            forward(number)

        done = number - start
        lax.fori_loop(done * PARTS // 3, (done + 1) * PARTS // 3, attention, 0)

        @pl.when((number == forwards - 1) & (inner == 1))
        def _():
            lax.fori_loop(held_from, held_to, send_back, 0)

        return carry

    lax.fori_loop(start, start + forwards, step_of, 0)
    def inputs_sent(index, carry):
        _, offset = split(index)
        for kind in range(3):
            for cut in range(CUTS):
                pair_copy(index, kind, cut).wait_send()

        @pl.when(offset != 0)
        def _():
            for kind in range(3):
                for cut in range(CUTS):
                    ring_copy(index, kind, cut).wait_send()

        return carry

    def outputs_sent(index, carry):
        _, offset = split(index)
        for part in range(PARTS):
            home_copy(index, part).wait_send()

        @pl.when(offset != 0)
        def _():
            for part in range(PARTS):
                back_copy(index, part).wait_send()

        return carry

    outer = half_units + lead
    final = stages - 1
    few = max(final - 1, 0)
    each(final, 1, 0, half_units - PARTS, send_home)
    each(few, final - few, outer, stage_units, send_home)
    lax.fori_loop(0, count, inputs_sent, 0)
    each(0, few, 0, stage_units, come_home)
    each(few, final - few, 0, outer, come_home)
    each(final, 1, half_units - PARTS, outer, come_home)
    each(final, 1, outer, stage_units, send_home)
    each(final, 1, 0, half_units - PARTS, come_home)
    each(few, stages - few, outer, stage_units, come_home)
    lax.fori_loop(0, count, outputs_sent, 0)


def paired_body(query_rows, key_rows, value_rows, cached_rows, plan, timestep, assignment):
    groups = lax.axis_size("batch")
    pieces = lax.axis_size("seq")
    _, rows, width = query_rows.shape
    stages = width // HEAD_DIM // (2 * pieces)
    count = stages * pieces
    smem = pl.BlockSpec(memory_space=pltpu.SMEM)
    anywhere = pl.BlockSpec(memory_space=pl.ANY)
    block = (rows, HEAD_DIM)
    return pl.pallas_call(
        functools.partial(kernel, groups, pieces, stages),
        out_shape=pltpu.VMEM(query_rows.shape, jnp.bfloat16),
        in_specs=[smem] * 3 + [anywhere] * 4,
        out_specs=pl.BlockSpec(memory_space=pltpu.VMEM),
        scratch_shapes=[
            pltpu.VMEM((3, rows, width // 2), jnp.bfloat16),
            pltpu.VMEM((3, count) + block, jnp.bfloat16),
            pltpu.VMEM((3, count) + block, jnp.bfloat16),
            pltpu.VMEM((3, stages, pieces * rows, HEAD_DIM), jnp.bfloat16),
            pltpu.VMEM((stages, pieces * rows, HEAD_DIM), jnp.bfloat16),
            pltpu.VMEM((count,) + block, jnp.bfloat16),
            pltpu.VMEM((count,) + block, jnp.bfloat16),
            pltpu.VMEM((rows, width), jnp.bfloat16),
            pltpu.SemaphoreType.DMA((3,)),
            pltpu.SemaphoreType.DMA((3, count)),
            pltpu.SemaphoreType.DMA,
            pltpu.SemaphoreType.DMA((3, count, CUTS)),
            pltpu.SemaphoreType.DMA((3, count, CUTS)),
            pltpu.SemaphoreType.DMA((3, count, CUTS)),
            pltpu.SemaphoreType.DMA((3, count, CUTS)),
            pltpu.SemaphoreType.DMA((count, PARTS)),
            pltpu.SemaphoreType.DMA((count, PARTS)),
            pltpu.SemaphoreType.DMA((count, PARTS)),
            pltpu.SemaphoreType.DMA((count, PARTS)),
        ],
        compiler_params=pltpu.CompilerParams(
            collective_id=0, has_side_effects=True, vmem_limit_bytes=56 << 20
        ),
    )(assignment, timestep, plan, query_rows, key_rows, value_rows, cached_rows)


def solution(mesh):
    placed = (
        P("batch", "seq", None),
        P("batch", "seq", None),
        P("batch", "seq", None),
        P("batch", "seq", None),
        P(),
        P(),
        P(),
    )
    groups, pieces = mesh.shape["batch"], mesh.shape["seq"]

    def body(query_rows, *rest):
        heads = query_rows.shape[2] // HEAD_DIM
        rows = query_rows.shape[1]
        even = groups % 2 == 0 and heads % (2 * pieces) == 0 and rows % (16 * PARTS * CUTS) == 0
        power = pieces > 1 and pieces & (pieces - 1) == 0
        chosen = paired_body if even and power else plain_body
        return chosen(query_rows, *rest)

    return jax.shard_map(
        body, mesh=mesh, in_specs=placed, out_specs=P("batch", "seq", None), check_vma=False
    )
```

```python
import functools
import math

import jax
import jax.numpy as jnp
from jax import lax
from jax.experimental import pallas as pl
from jax.experimental.pallas import tpu as pltpu
from jax.sharding import PartitionSpec as P

HEAD_DIM = 128
MESH = pl.DeviceIdType.MESH
PARTS = 4
CUTS = 1
DELAY = 3
ORDER = ((1, 0), (2, 0), (1, 1), (2, 1), (0, 0), (0, 1))


def block_rows(row_count):
    for candidate in range(512, row_count + 1):
        if row_count % candidate == 0:
            return candidate
    return row_count


def attend(head_queries, head_keys, head_values):
    row_count, head_count, depth = head_queries.shape
    block = block_rows(row_count)
    factor = 1.0 / math.sqrt(depth)
    stacked = head_queries.reshape(row_count // block, block, head_count, depth)

    def one_block(query_block):
        scores = (
            jnp.einsum("qnd,knd->nqk", query_block, head_keys, preferred_element_type=jnp.float32)
            * factor
        )
        peak = jnp.max(scores, axis=2, keepdims=True)
        shifted = jnp.exp(scores - peak)
        total = jnp.sum(shifted, axis=2)
        weights = shifted.astype(jnp.bfloat16)
        mixed = jnp.einsum("nqk,knd->qnd", weights, head_values, preferred_element_type=jnp.float32)
        return (mixed / jnp.transpose(total)[:, :, None]).astype(jnp.bfloat16)

    return lax.map(one_block, stacked).reshape(row_count, head_count, depth)


def skipped(head_queries, head_keys, head_values):
    return jnp.zeros(head_queries.shape, jnp.bfloat16)


def plain_body(query_rows, key_rows, value_rows, cached_rows, plan, timestep, assignment):
    pieces = lax.axis_size("seq")
    local_rows = query_rows.shape[1]
    width = query_rows.shape[2]
    group = lax.axis_index("batch")
    slot_index = jnp.arange(assignment.shape[0], dtype=jnp.int32)
    request = jnp.sum(jnp.where(slot_index == group, assignment, 0))
    moment = jnp.sum(jnp.where(slot_index == request, timestep, 0))
    step_index = jnp.arange(plan.shape[1], dtype=jnp.int32)
    chosen = (slot_index[:, None] == request) & (step_index[None, :] == moment)
    active = jnp.sum(jnp.where(chosen, plan, 0)) > 0

    def arrange(rows):
        return rows[0].reshape(local_rows, pieces, width // (pieces * HEAD_DIM), HEAD_DIM)

    def gather(rows):
        return lax.all_to_all(arrange(rows), "seq", split_axis=1, concat_axis=0, tiled=True)[:, 0]

    attended = lax.cond(
        active, attend, skipped, gather(query_rows), gather(key_rows), gather(value_rows)
    )
    moved = lax.all_to_all(attended[:, None], "seq", split_axis=0, concat_axis=1, tiled=True)
    fresh = moved.reshape(1, local_rows, width)
    return jnp.where(active, fresh, cached_rows)


def exclusive(number, other, size):
    total = 0
    bit = 1
    while bit < size:
        total = total + bit * ((number // bit + other // bit) % 2)
        bit *= 2
    return total


def kernel(
    groups, pieces, stages,
    assignment_ref, timestep_ref, plan_ref, query_ref, key_ref, value_ref, cached_ref,
    out_ref,
    own, other, paired, gathered, mixed, backs, homes, cached,
    own_sem, other_sem, cached_sem, pair_send, pair_recv, ring_send, ring_recv,
    back_send, back_recv, home_send, home_recv,
):
    batch = lax.axis_index("batch")
    me = lax.axis_index("seq")
    half = groups // 2
    side = batch // half
    partner = (batch + half) % groups
    other_side = 1 - side
    rows = query_ref.shape[1]
    count = stages * pieces
    sources = (query_ref, key_ref, value_ref)

    request = assignment_ref[batch]
    moment = timestep_ref[request]
    active = plan_ref[request, moment] > 0

    def split(index):
        return index // pieces, pieces - 1 - index % pieces

    def columns(which, peer, stage):
        head = (which * pieces + peer) * stages + stage
        return pl.ds(pl.multiple_of(head * HEAD_DIM, HEAD_DIM), HEAD_DIM)

    def rows_of(peer):
        return pl.ds(pl.multiple_of(peer * rows, rows), rows)

    share = rows // PARTS
    slab = rows // CUTS

    def part_rows(part, peer=0):
        return pl.ds(pl.multiple_of(peer * rows + part * share, share), share)

    def cut_rows(cut, peer=0):
        return pl.ds(pl.multiple_of(peer * rows + cut * slab, slab), slab)

    def other_copy(index, kind):
        stage, offset = split(index)
        peer = exclusive(me, offset, pieces)
        return pltpu.make_async_copy(
            sources[kind].at[0, :, columns(other_side, peer, stage)],
            other.at[kind, index],
            other_sem.at[kind, index],
        )

    def pair_copy(index, kind, cut):
        return pltpu.make_async_remote_copy(
            src_ref=other.at[kind, index, cut_rows(cut)],
            dst_ref=paired.at[kind, index, cut_rows(cut)],
            send_sem=pair_send.at[kind, index, cut],
            recv_sem=pair_recv.at[kind, index, cut],
            device_id=(partner, me),
            device_id_type=MESH,
        )

    def ring_copy(index, kind, cut):
        stage, offset = split(index)
        peer = exclusive(me, offset, pieces)
        return pltpu.make_async_remote_copy(
            src_ref=paired.at[kind, index, cut_rows(cut)],
            dst_ref=gathered.at[kind, stage, cut_rows(cut, me)],
            send_sem=ring_send.at[kind, index, cut],
            recv_sem=ring_recv.at[kind, index, cut],
            device_id=(batch, peer),
            device_id_type=MESH,
        )

    def back_copy(index, part):
        stage, offset = split(index)
        peer = exclusive(me, offset, pieces)
        return pltpu.make_async_remote_copy(
            src_ref=mixed.at[stage, part_rows(part, peer)],
            dst_ref=backs.at[index, part_rows(part)],
            send_sem=back_send.at[index, part],
            recv_sem=back_recv.at[index, part],
            device_id=(batch, peer),
            device_id_type=MESH,
        )

    def home_copy(index, part):
        return pltpu.make_async_remote_copy(
            src_ref=backs.at[index, part_rows(part)],
            dst_ref=homes.at[index, part_rows(part)],
            send_sem=home_send.at[index, part],
            recv_sem=home_recv.at[index, part],
            device_id=(partner, me),
            device_id_type=MESH,
        )

    def settle(index, part, which, fresh):
        stage, offset = split(index)
        lanes = columns(which, exclusive(me, offset, pieces), stage)
        where = part_rows(part)
        out_ref[0, where, lanes] = lax.select_n(active, cached[where, lanes], fresh[index, where])

    def own_copy(kind):
        width = pieces * stages * HEAD_DIM
        start = pl.multiple_of(side * width, HEAD_DIM)
        return pltpu.make_async_copy(
            sources[kind].at[0, :, pl.ds(start, width)], own.at[kind], own_sem.at[kind]
        )

    barrier = pltpu.get_barrier_semaphore()
    pl.semaphore_signal(barrier, inc=1, device_id=(partner, me), device_id_type=MESH)
    for step in range(1, pieces):
        pl.semaphore_signal(
            barrier, inc=1, device_id=(batch, (me + step) % pieces), device_id_type=MESH
        )

    def load_others(group, carry):
        for kind, sub in ORDER:
            other_copy(2 * group + sub, kind).start()
        return carry

    lax.fori_loop(0, count // 2, load_others, 0)
    for kind in (1, 2, 0):
        own_copy(kind).start()
    pl.semaphore_wait(barrier, pieces)

    per_stage = 3 * pieces
    forwards = stages * per_stage
    stage_units = pieces * PARTS
    units = stages * stage_units
    start = per_stage + min(DELAY, 3 * (pieces // 2 - 1))
    held_from = max(stages - 2, 0) * stage_units
    held_to = held_from + stage_units // 2 * (stages > 1)
    half_units = stage_units // 2
    lead = half_units // 2
    inner = (me + 1) // 2 % 2

    def start_pairs(group, carry):
        for kind, sub in ORDER:
            other_copy(2 * group + sub, kind).wait()
            for cut in range(CUTS):
                pair_copy(2 * group + sub, kind, cut).start()
        return carry

    start_pairs(0, 0)
    cached_copy = pltpu.make_async_copy(cached_ref.at[0], cached, cached_sem)
    cached_copy.start()
    for kind in range(3):
        own_copy(kind).wait()

    def forward(number):
        place = number % 6

        @pl.when((place == 0) & (number < forwards - 6))
        def _():
            start_pairs(number // 6 + 1, 0)

        late = place // 4
        kind = (1 - late) * (1 + place % 2)
        index = number // 6 * 2 + (1 - late) * (place // 2) + late * (place - 4)
        stage, offset = split(index)
        peer = exclusive(me, offset, pieces)
        lanes = pl.ds(pl.multiple_of((peer * stages + stage) * HEAD_DIM, HEAD_DIM), HEAD_DIM)
        for cut in range(CUTS):
            pair_copy(index, kind, cut).wait_recv()
            mine = own[kind, cut_rows(cut), lanes]
            chosen = lax.select_n(active, paired[kind, index, cut_rows(cut)], mine)

            @pl.when(offset != 0)
            def _():
                paired[kind, index, cut_rows(cut)] = chosen
                ring_copy(index, kind, cut).start()

            @pl.when(offset == 0)
            def _():
                gathered[kind, stage, cut_rows(cut, me), :] = chosen

    def send_back(unit, carry):
        index, part = unit // PARTS, unit % PARTS
        _, offset = split(index)

        @pl.when(offset != 0)
        def _():
            back_copy(index, part).start()

        return carry

    def unit_of(stage, place):
        crossing = place // half_units
        turned = (place + inner * (half_units // 2)) % half_units
        within = crossing * turned + (1 - crossing) * (half_units + place)
        unit = stage * stage_units + within
        return unit // PARTS, unit % PARTS

    def send_home(stage, place):
        index, part = unit_of(stage, place)
        _, offset = split(index)

        @pl.when(offset != 0)
        def _():
            back_copy(index, part).wait_recv()

        home_copy(index, part).start()
        settle(index, part, side, backs)

    def come_home(stage, place):
        index, part = unit_of(stage, place)
        home_copy(index, part).wait_recv()
        settle(index, part, other_side, homes)

    def each(first, number, low, high, action):
        span = high - low

        def body(item, carry):
            action(first + item // span, low + item % span)
            return carry

        lax.fori_loop(0, number * span, body, 0)

    def attention(unit, carry):
        turn, part = unit // PARTS, unit % PARTS
        index = turn // pieces * pieces + (turn + pieces - 1) % pieces
        stage, offset = split(index)
        peer = exclusive(me, offset, pieces)

        @pl.when((unit % stage_units == 0) & (stage > 0))
        def _():
            each(stage - 1, 1, 0, half_units - PARTS, send_home)

        @pl.when(unit % stage_units == 0)
        def _():
            def arrived(step, carry):
                for kind in (1, 2):
                    for cut in range(CUTS):
                        ring_copy(stage * pieces + step, kind, cut).wait_recv()
                return carry

            lax.fori_loop(0, pieces - 1, arrived, 0)

            @pl.when((unit == units - stage_units) & (inner == 0))
            def _():
                lax.fori_loop(held_from, held_to, send_back, 0)

        @pl.when((offset != 0) & (part == 0))
        def _():
            for cut in range(CUTS):
                ring_copy(index, 0, cut).wait_recv()

        factor = math.log2(math.e) / math.sqrt(HEAD_DIM)
        where = part_rows(part, peer)
        queries = gathered[0, stage, where, :]
        scores = lax.dot_general(
            queries, gathered[1, stage], (((1,), (1,)), ((), ())),
            preferred_element_type=jnp.float32,
        )
        peak = jnp.max(scores, axis=1, keepdims=True)
        weights = jnp.exp2((scores - peak) * factor)
        total = jnp.sum(weights, axis=1, keepdims=True)
        result = jnp.dot(
            weights.astype(jnp.bfloat16), gathered[2, stage], preferred_element_type=jnp.float32
        )
        blended = (result / total).astype(jnp.bfloat16)

        @pl.when(offset != 0)
        def _():
            mixed[stage, where, :] = blended

        @pl.when(offset == 0)
        def _():
            backs[index, part_rows(part)] = blended
            home_copy(index, part).start()
            settle(index, part, side, backs)

        @pl.when((stage != stages - 2) | (offset < pieces // 2))
        def _():
            send_back(index * PARTS + part, 0)

        spot = unit % stage_units

        @pl.when((stage > 0) & (spot >= half_units) & (unit < units - lead))
        def _():
            send_home(stage - 1, spot)

        @pl.when(unit >= units - lead)
        def _():
            send_home(stage, spot - lead)

        return carry

    def early(number, carry):
        forward(number)
        return carry

    lax.fori_loop(0, min(start, forwards), early, 0)
    cached_copy.wait()

    def step_of(number, carry):
        @pl.when(number < forwards)
        def _():
            forward(number)

        done = number - start
        lax.fori_loop(done * PARTS // 3, (done + 1) * PARTS // 3, attention, 0)

        @pl.when((number == forwards - 1) & (inner == 1))
        def _():
            lax.fori_loop(held_from, held_to, send_back, 0)

        return carry

    lax.fori_loop(start, start + forwards, step_of, 0)
    def inputs_sent(index, carry):
        _, offset = split(index)
        for kind in range(3):
            for cut in range(CUTS):
                pair_copy(index, kind, cut).wait_send()

        @pl.when(offset != 0)
        def _():
            for kind in range(3):
                for cut in range(CUTS):
                    ring_copy(index, kind, cut).wait_send()

        return carry

    def outputs_sent(index, carry):
        _, offset = split(index)
        for part in range(PARTS):
            home_copy(index, part).wait_send()

        @pl.when(offset != 0)
        def _():
            for part in range(PARTS):
                back_copy(index, part).wait_send()

        return carry

    outer = half_units + lead
    final = stages - 1
    few = max(final - 1, 0)
    each(final, 1, 0, half_units - PARTS, send_home)
    each(few, final - few, outer, stage_units, send_home)
    lax.fori_loop(0, count, inputs_sent, 0)
    each(0, few, 0, stage_units, come_home)
    each(few, final - few, 0, outer, come_home)
    each(final, 1, outer, stage_units, send_home)
    each(final, 1, half_units - PARTS, outer, come_home)
    each(final, 1, 0, half_units - PARTS, come_home)
    each(few, stages - few, outer, stage_units, come_home)
    lax.fori_loop(0, count, outputs_sent, 0)


def paired_body(query_rows, key_rows, value_rows, cached_rows, plan, timestep, assignment):
    groups = lax.axis_size("batch")
    pieces = lax.axis_size("seq")
    _, rows, width = query_rows.shape
    stages = width // HEAD_DIM // (2 * pieces)
    count = stages * pieces
    smem = pl.BlockSpec(memory_space=pltpu.SMEM)
    anywhere = pl.BlockSpec(memory_space=pl.ANY)
    block = (rows, HEAD_DIM)
    return pl.pallas_call(
        functools.partial(kernel, groups, pieces, stages),
        out_shape=pltpu.VMEM(query_rows.shape, jnp.bfloat16),
        in_specs=[smem] * 3 + [anywhere] * 4,
        out_specs=pl.BlockSpec(memory_space=pltpu.VMEM),
        scratch_shapes=[
            pltpu.VMEM((3, rows, width // 2), jnp.bfloat16),
            pltpu.VMEM((3, count) + block, jnp.bfloat16),
            pltpu.VMEM((3, count) + block, jnp.bfloat16),
            pltpu.VMEM((3, stages, pieces * rows, HEAD_DIM), jnp.bfloat16),
            pltpu.VMEM((stages, pieces * rows, HEAD_DIM), jnp.bfloat16),
            pltpu.VMEM((count,) + block, jnp.bfloat16),
            pltpu.VMEM((count,) + block, jnp.bfloat16),
            pltpu.VMEM((rows, width), jnp.bfloat16),
            pltpu.SemaphoreType.DMA((3,)),
            pltpu.SemaphoreType.DMA((3, count)),
            pltpu.SemaphoreType.DMA,
            pltpu.SemaphoreType.DMA((3, count, CUTS)),
            pltpu.SemaphoreType.DMA((3, count, CUTS)),
            pltpu.SemaphoreType.DMA((3, count, CUTS)),
            pltpu.SemaphoreType.DMA((3, count, CUTS)),
            pltpu.SemaphoreType.DMA((count, PARTS)),
            pltpu.SemaphoreType.DMA((count, PARTS)),
            pltpu.SemaphoreType.DMA((count, PARTS)),
            pltpu.SemaphoreType.DMA((count, PARTS)),
        ],
        compiler_params=pltpu.CompilerParams(
            collective_id=0, has_side_effects=True, vmem_limit_bytes=56 << 20
        ),
    )(assignment, timestep, plan, query_rows, key_rows, value_rows, cached_rows)


def solution(mesh):
    placed = (
        P("batch", "seq", None),
        P("batch", "seq", None),
        P("batch", "seq", None),
        P("batch", "seq", None),
        P(),
        P(),
        P(),
    )
    groups, pieces = mesh.shape["batch"], mesh.shape["seq"]

    def body(query_rows, *rest):
        heads = query_rows.shape[2] // HEAD_DIM
        rows = query_rows.shape[1]
        even = groups % 2 == 0 and heads % (2 * pieces) == 0 and rows % (16 * PARTS * CUTS) == 0
        power = pieces > 1 and pieces & (pieces - 1) == 0
        chosen = paired_body if even and power else plain_body
        return chosen(query_rows, *rest)

    return jax.shard_map(
        body, mesh=mesh, in_specs=placed, out_specs=P("batch", "seq", None), check_vma=False
    )
```
